32 devices in a mesh: outer: 4 (over y, core), atoms: 8 (over z, x).
Axes of the slice: x: 2, y: 2, z: 4, core: 2. Of those that a mesh axis runs over, the one named last changes fastest.
Arguments:
- features: float32 [32768, 128], P(('outer', 'atoms')), may hold values from -6 to 6
- positions: int32 [3, 32768], P(None, ('outer', 'atoms')), may hold values from 0 to 262143
- wavevectors: int32 [3, 768], replicated, may hold values from -6 to 6
- w_value: float32 [2, 128, 128], replicated, may hold values from -0.5 to 0.5
- freq_filter: float32 [2, 768, 128], replicated, may hold values from 0.05 to 1
- norm_gain: float32 [2, 128], replicated, may hold values from 0.1 to 1.9
- w_hidden: float32 [2, 128, 128], replicated, may hold values from -0.5 to 0.5
- b_hidden: float32 [2, 128], replicated, may hold values from -4 to 4
- w_output: float32 [2, 128, 128], replicated, may hold values from -0.5 to 0.5
Outputs:
- updated: float32 [32768, 128], P(('outer', 'atoms'))
The draws below stay inside these ranges and needn't reach their ends.
All inputs are finite; a program needn't handle non-finite values.
Results may differ from the reference program's by a relative error of at most 0.0003.
Values sent between devices are 32-bit elements; how exact they have to be, the bound alone decides.
No kernel may reach another device: no remote copies, remote signals or barrier semaphores. Data moves between devices by JAX's collectives and lax.ppermute only.
A program may use at most 64 MiB of HBM per device.

```python
import math
import jax
import jax.numpy as jnp
from jax import lax

ATOM_DEV = 1024
CHANNELS = 128
WAVES = 768
BLOCKS = 2
ATOMS = 32768


def place_ends(result, own_key, low, largest):
    shape = result.shape
    index_at = [jax.random.randint(jax.random.fold_in(own_key, axis), (), 0, shape[axis]) for axis in range(len(shape))]
    result = result.at[tuple(index_at)].set(low)
    longest = shape.index(max(shape))
    index_at[longest] = (index_at[longest] + 1) % shape[longest]
    return result.at[tuple(index_at)].set(largest)


def steps_of(own_key, extent, cuts, smallest, high):
    level, own = 1.0, jax.random.fold_in(own_key, 6)
    for axis_at, shards_of in cuts:
        draws = jnp.exp(jax.random.uniform(jax.random.fold_in(own, axis_at), (shards_of,), jnp.float32, smallest / len(cuts), high / len(cuts)))
        level = level * jnp.repeat(draws, extent[axis_at] // shards_of).reshape([-1 if axis == axis_at else 1 for axis in range(len(extent))])
    return level


def normal_values(rng, extent, deviation, most, pieces=(), held_as=jnp.bfloat16):
    drawn = deviation * jax.random.normal(rng, extent, jnp.float32)
    if pieces:
        drawn = drawn * steps_of(rng, extent, pieces, -0.22, 0.18)
    return jnp.clip(drawn, -most, most).astype(held_as)


def setup_inputs(seed: int = 0) -> dict:
    arg_keys = jax.random.split(jax.random.key(seed), 10)
    return {
        "features": normal_values(arg_keys[0], (ATOMS, CHANNELS), 1.0, 6.0, ((0, 32),), jnp.float32),
        "positions": place_ends(jax.random.randint(arg_keys[1], (3, ATOMS), 0, 262144), jax.random.fold_in(arg_keys[1], 1), 0, 262143).astype(jnp.int32),
        "wavevectors": place_ends(jax.random.randint(arg_keys[2], (3, WAVES), -6, 7), jax.random.fold_in(arg_keys[2], 1), -6, 6).astype(jnp.int32),
        "w_value": normal_values(arg_keys[3], (BLOCKS, CHANNELS, CHANNELS), CHANNELS ** -0.5, 0.5, (), jnp.float32),
        "freq_filter": jnp.clip(jnp.exp(jax.random.uniform(arg_keys[4], (BLOCKS, WAVES, CHANNELS), jnp.float32, math.log(0.05), math.log(1.0))), 0.05, 1.0),
        "norm_gain": jnp.clip(1.0 + 0.18 * jax.random.normal(arg_keys[5], (BLOCKS, CHANNELS), jnp.float32), 0.1, 1.9),
        "w_hidden": normal_values(arg_keys[6], (BLOCKS, CHANNELS, CHANNELS), CHANNELS ** -0.5, 0.5, (), jnp.float32),
        "b_hidden": normal_values(arg_keys[7], (BLOCKS, CHANNELS), 1.0, 4.0, (), jnp.float32),
        "w_output": normal_values(arg_keys[8], (BLOCKS, CHANNELS, CHANNELS), CHANNELS ** -0.5, 0.5, (), jnp.float32),
    }


fixed_scale = 262144
highest = lax.Precision.HIGHEST

def phases(pos_block, wave_block):
    integer_dot = pos_block[0][:, None] * wave_block[0][None, :]
    integer_dot = integer_dot + pos_block[1][:, None] * wave_block[1][None, :]
    integer_dot = integer_dot + pos_block[2][:, None] * wave_block[2][None, :]
    wrapped = jnp.mod(integer_dot, fixed_scale).astype(jnp.int32)
    return wrapped.astype(jnp.float32) * (2.0 * math.pi / fixed_scale)

def reference(features, positions, wavevectors, w_value, freq_filter, norm_gain, w_hidden, b_hidden, w_output):
    current = features
    pos_blocks = positions.reshape(3, -1, ATOM_DEV).transpose(1, 0, 2)
    for layer_index in range(BLOCKS):
        projected = jnp.dot(current, w_value[layer_index], precision=highest, preferred_element_type=jnp.float32)
        value_blocks = projected.reshape(-1, ATOM_DEV, CHANNELS)

        def accumulate(running, block_item):
            pos_block, value_block = block_item
            angles = phases(pos_block, wavevectors)
            real_part = jnp.einsum('ak,ac->kc', jnp.cos(angles), value_block, precision=highest)
            imag_part = -jnp.einsum('ak,ac->kc', jnp.sin(angles), value_block, precision=highest)
            return (running + jnp.concatenate([real_part, imag_part], axis=1), None)
        factor, _ = lax.scan(accumulate, jnp.zeros((WAVES, 2 * CHANNELS), jnp.float32), (pos_blocks, value_blocks))
        filtered = factor * jnp.concatenate([freq_filter[layer_index], freq_filter[layer_index]], axis=1)

        def back_project(pos_block):
            angles = phases(pos_block, wavevectors)
            first = jnp.dot(jnp.cos(angles), filtered[:, :CHANNELS], precision=highest, preferred_element_type=jnp.float32)
            second = jnp.dot(jnp.sin(angles), filtered[:, CHANNELS:], precision=highest, preferred_element_type=jnp.float32)
            return first - second
        messages = lax.map(back_project, pos_blocks).reshape(-1, CHANNELS)
        normed = messages * lax.rsqrt(lax.optimization_barrier(jnp.mean(messages * messages, axis=1, keepdims=True)) + 1e-06) * norm_gain[layer_index]
        hidden = jax.nn.silu(jnp.dot(normed, w_hidden[layer_index], precision=highest, preferred_element_type=jnp.float32) + b_hidden[layer_index])
        current = current + jnp.dot(hidden, w_output[layer_index], precision=highest, preferred_element_type=jnp.float32)
    return current
```

```python
import math

import jax
import jax.numpy as jnp
from jax import lax
from jax.sharding import PartitionSpec as P

fixed_scale = 262144
highest = lax.Precision.HIGHEST
axes = ("outer", "atoms")


def phases(pos_block, wave_block):
    integer_dot = pos_block[0][:, None] * wave_block[0][None, :]
    integer_dot = integer_dot + pos_block[1][:, None] * wave_block[1][None, :]
    integer_dot = integer_dot + pos_block[2][:, None] * wave_block[2][None, :]
    wrapped = jnp.mod(integer_dot, fixed_scale)
    return wrapped.astype(jnp.float32) * (2.0 * math.pi / fixed_scale)


class Layout:
    def __init__(self, mesh):
        self.outer, self.atoms = mesh.shape["outer"], mesh.shape["atoms"]
        self.pair = 2 if self.outer % 2 == 0 else 1
        self.high = self.outer // self.pair
        self.low = 2 if self.atoms % 2 == 0 else 1
        self.line = self.atoms // self.low
        self.square = self.high * self.low
        self.chunks = self.pair * self.square

    def split(self, index):
        outer, atoms = index // self.atoms, index % self.atoms
        return outer // self.pair, outer % self.pair, atoms // self.low, atoms % self.low

    def join(self, high, pair, line, low):
        return (high * self.pair + pair) * self.atoms + line * self.low + low

    def moved(self, index, d_high, d_pair, d_line, d_low):
        high, pair, line, low = self.split(index)
        return self.join(
            (high + d_high) % self.high,
            (pair + d_pair) % self.pair,
            (line + d_line) % self.line,
            (low + d_low) % self.low,
        )

    def send(self, value, **steps):
        d = dict(d_high=0, d_pair=0, d_line=0, d_low=0) | steps
        count = self.outer * self.atoms
        return lax.ppermute(value, axes, [(i, self.moved(i, **d)) for i in range(count)])

    def owned(self):
        outer, atoms = lax.axis_index("outer"), lax.axis_index("atoms")
        return outer % self.pair, outer // self.pair, atoms % self.low

    def chunk_of(self, d_pair, d_high, d_low):
        pair, high, low = self.owned()
        pair = (pair + d_pair) % self.pair
        high = (high + d_high) % self.high
        low = (low + d_low) % self.low
        return (pair * self.high + high) * self.low + low

    def offsets(self):
        return [(p, h, w) for p in range(self.pair) for h in range(self.high) for w in range(self.low)]


def total(layout, parts, scale):
    squares = [(h, w) for h in range(layout.high) for w in range(layout.low)]
    held = {}
    for h, w in squares[1:] + squares[:1]:
        value = parts[0, h, w]
        for p in range(1, layout.pair):
            value = value + layout.send(parts[p, h, w], d_pair=p)
        held[h, w] = value
    own = held[0, 0]
    for h, w in squares[1:]:
        own = own + layout.send(held[h, w], d_high=h, d_low=w)
    if layout.line <= 4:
        summed = own
        for d in range(1, layout.line):
            summed = summed + layout.send(own, d_line=d)
    else:
        summed, span = own, 1
        while span < layout.line:
            summed = summed + layout.send(summed, d_line=span)
            span *= 2
    own = summed * scale
    out = {}
    for h, w in squares:
        value = own if (h, w) == (0, 0) else layout.send(own, d_high=-h, d_low=-w)
        out[0, h, w] = value
        for p in range(1, layout.pair):
            out[p, h, w] = layout.send(value, d_pair=-p)
    return out


def local(
    layout, features, positions, wavevectors, w_value, freq_filter, norm_gain, w_hidden, b_hidden, w_output
):
    wave_count = wavevectors.shape[1]
    channel_count = features.shape[1]
    rows = wave_count // layout.chunks
    offsets = layout.offsets()
    wave_chunks = wavevectors.reshape(3, layout.chunks, rows)
    cos_parts, sin_parts = [], []
    for offset in offsets:
        chunk = lax.dynamic_index_in_dim(wave_chunks, layout.chunk_of(*offset), 1, keepdims=False)
        angles = phases(positions, chunk)
        cos_parts.append(jnp.cos(angles))
        sin_parts.append(jnp.sin(angles))
    cos_table = jnp.concatenate(cos_parts, axis=1)
    sin_table = jnp.concatenate(sin_parts, axis=1)
    own_rows = layout.chunk_of(0, 0, 0) * rows
    current = features
    for layer_index in range(w_value.shape[0]):
        projected = jnp.dot(
            current, w_value[layer_index], precision=highest, preferred_element_type=jnp.float32
        )
        real_part = jnp.einsum("ak,ac->kc", cos_table, projected, precision=highest)
        imag_part = -jnp.einsum("ak,ac->kc", sin_table, projected, precision=highest)
        factor = jnp.concatenate([real_part, imag_part], axis=1)
        own_filter = lax.dynamic_slice_in_dim(freq_filter[layer_index], own_rows, rows, 0)
        scale = jnp.concatenate([own_filter, own_filter], axis=1)
        parts = {o: factor[n * rows : (n + 1) * rows] for n, o in enumerate(offsets)}
        gathered = total(layout, parts, scale)
        filtered = jnp.concatenate([gathered[o] for o in offsets], axis=0)
        messages = jnp.dot(
            cos_table,
            filtered[:, :channel_count],
            precision=highest,
            preferred_element_type=jnp.float32,
        )
        messages = messages - jnp.dot(
            sin_table,
            filtered[:, channel_count:],
            precision=highest,
            preferred_element_type=jnp.float32,
        )
        normed = (
            messages
            * lax.rsqrt(jnp.mean(messages * messages, axis=1, keepdims=True) + 1e-06)
            * norm_gain[layer_index]
        )
        hidden = jax.nn.silu(
            jnp.dot(
                normed, w_hidden[layer_index], precision=highest, preferred_element_type=jnp.float32
            )
            + b_hidden[layer_index]
        )
        current = current + jnp.dot(
            hidden, w_output[layer_index], precision=highest, preferred_element_type=jnp.float32
        )
    return current


def solution(mesh):
    placed = (
        P(("outer", "atoms"), None),
        P(None, ("outer", "atoms")),
        P(),
        P(),
        P(),
        P(),
        P(),
        P(),
        P(),
    )
    layout = Layout(mesh)

    def body(*arguments):
        return local(layout, *arguments)

    return jax.shard_map(
        body, mesh=mesh, in_specs=placed, out_specs=P(("outer", "atoms"), None), check_vma=False
    )
```

```python
import jax
import jax.numpy as jnp
from jax import lax
from jax.experimental import pallas as pl
from jax.experimental.pallas import tpu as pltpu
from jax.sharding import PartitionSpec as P

axes = ("outer", "atoms")
turn_bits = 18
half_sin = (0.10982699, -0.84611289, 3.60635441, -7.3082457, 4.44288292)
half_cos = (0.31069819, -1.88356299, 5.73946117, -6.97885099, 1.4142135)
f32, bf16 = jnp.float32, jnp.bfloat16


class Layout:
    def __init__(self, mesh):
        self.outer, self.atoms = mesh.shape["outer"], mesh.shape["atoms"]
        self.pair = 2 if self.outer % 2 == 0 else 1
        self.high = self.outer // self.pair
        self.low = 2 if self.atoms % 2 == 0 else 1
        self.line = self.atoms // self.low
        self.square = self.high * self.low
        self.chunks = self.pair * self.square

    def split(self, index):
        outer, atoms = index // self.atoms, index % self.atoms
        return outer // self.pair, outer % self.pair, atoms // self.low, atoms % self.low

    def join(self, high, pair, line, low):
        return (high * self.pair + pair) * self.atoms + line * self.low + low

    def moved(self, index, d_high, d_pair, d_line, d_low):
        high, pair, line, low = self.split(index)
        return self.join(
            (high + d_high) % self.high,
            (pair + d_pair) % self.pair,
            (line + d_line) % self.line,
            (low + d_low) % self.low,
        )

    def send(self, value, **steps):
        d = dict(d_high=0, d_pair=0, d_line=0, d_low=0) | steps
        count = self.outer * self.atoms
        return lax.ppermute(value, axes, [(i, self.moved(i, **d)) for i in range(count)])

    def owned(self):
        outer, atoms = lax.axis_index("outer"), lax.axis_index("atoms")
        return outer % self.pair, outer // self.pair, atoms % self.low

    def chunk_of(self, d_pair, d_high, d_low):
        pair, high, low = self.owned()
        pair = (pair + d_pair) % self.pair
        high = (high + d_high) % self.high
        low = (low + d_low) % self.low
        return (pair * self.high + high) * self.low + low

    def offsets(self):
        return [(p, h, w) for p in range(self.pair) for h in range(self.high) for w in range(self.low)]


def total(layout, parts, scale):
    squares = [(h, w) for h in range(layout.high) for w in range(layout.low)]
    held = {}
    for h, w in squares[1:] + squares[:1]:
        value = parts[0, h, w]
        for p in range(1, layout.pair):
            value = value + layout.send(parts[p, h, w], d_pair=p)
        held[h, w] = value
    own = held[0, 0]
    for h, w in squares[1:]:
        own = own + layout.send(held[h, w], d_high=h, d_low=w)
    if layout.line <= 4:
        summed = own
        for d in range(1, layout.line):
            summed = summed + layout.send(own, d_line=d)
    else:
        summed, span = own, 1
        while span < layout.line:
            summed = summed + layout.send(summed, d_line=span)
            span *= 2
    own = summed * scale
    out = {}
    for h, w in squares:
        value = own if (h, w) == (0, 0) else layout.send(own, d_high=-h, d_low=-w)
        out[0, h, w] = value
        for p in range(1, layout.pair):
            out[p, h, w] = layout.send(value, d_pair=-p)
    return out


def halves(value):
    high = value.astype(bf16)
    return high, (value - high.astype(f32)).astype(bf16)


def matmul(left, right):
    return jnp.dot(left, right, preferred_element_type=f32)


def paired(value):
    high, low = halves(value)
    return jnp.concatenate([high, low], axis=1)


def product(left, right):
    width = right.shape[1]
    left_high, left_low = halves(left)
    pair = paired(right)
    both = matmul(left_high, pair)
    return both[:, :width] + both[:, width:] + matmul(left_low, pair[:, :width])


def digits(position):
    return (
        (position >> 12).astype(f32) * 2.0**-6,
        ((position >> 6) & 63).astype(f32) * 2.0**-12,
        (position & 63).astype(f32) * 2.0**-turn_bits,
    )


def operands(waves_ref, positions_ref, wave_rows, digit_rows):
    wave_rows[...] = jnp.zeros_like(wave_rows)
    digit_rows[...] = jnp.zeros_like(digit_rows)
    waves = waves_ref[...].astype(f32)
    for n, digit in enumerate(digits(positions_ref[...])):
        wave_rows[3 * n : 3 * n + 3, :] = waves
        digit_rows[3 * n : 3 * n + 3, :] = digit


def contract_rows(left, right):
    return lax.dot_general(
        left.astype(bf16), right.astype(bf16), (((0,), (0,)), ((), ())), preferred_element_type=f32
    )


def horner(coefficients, u):
    value = coefficients[0] * u + coefficients[1]
    for c in coefficients[2:]:
        value = value * u + c
    return value


def fill_tables(turns_ref, cos_high, cos_low, sin_high, sin_low):
    rows, columns = turns_ref.shape
    step, width = 32, 256

    def body(n, carry):
        here = pl.ds(pl.multiple_of(n * step, step), step)
        for at in range(0, columns, width):
            lanes = slice(at, at + width)
            turns = turns_ref[here, lanes]
            t = turns - jnp.round(turns)
            u = t * t
            s = horner(half_sin, u) * t
            c = horner(half_cos, u)
            cos_high[here, lanes], cos_low[here, lanes] = halves(1.0 - s * s)
            sin_high[here, lanes], sin_low[here, lanes] = halves(s * c)
        return carry

    lax.fori_loop(0, rows // step, body, 0)


def project(layout, tables, pair, chunk_refs, rows):
    width = pair.shape[1] // 2
    for offset, chunk_ref in zip(layout.offsets(), chunk_refs):
        here = pl.ds(pl.multiple_of(layout.chunk_of(*offset) * rows, rows), rows)
        for n in range(2):
            both = matmul(tables[2 * n][here, :], pair)
            rest = matmul(tables[2 * n + 1][here, :], pair[:, :width])
            chunk_ref[n * rows : (n + 1) * rows, :] = both[:, :width] + both[:, width:] + rest


def first_kernel(layout, rows, waves, positions, features, w_value, *refs):
    tables, chunks = refs[:4], refs[4 : 4 + layout.chunks]
    wave_rows, digit_rows, turns = refs[4 + layout.chunks :]
    operands(waves, positions, wave_rows, digit_rows)
    turns[...] = contract_rows(wave_rows[...], digit_rows[...])
    fill_tables(turns, *tables)
    pair = paired(product(features[...], w_value[0]))
    project(layout, tables, pair, chunks, rows)


def atom_table_kernel(waves, positions, *refs):
    tables = refs[:4]
    wave_rows, digit_rows, turns = refs[4:]
    operands(waves, positions, wave_rows, digit_rows)
    turns[...] = contract_rows(digit_rows[...], wave_rows[...])
    fill_tables(turns, *tables)


def block_kernel(layout, rows, block, last, *refs):
    chunks_in, refs = refs[: layout.chunks], refs[layout.chunks :]
    atom_tables, refs = refs[:4], refs[4:]
    current_ref, gain, w_hidden, b_hidden, w_output = refs[:5]
    refs = refs[5:]
    if not last:
        w_value, tables, refs = refs[0], refs[1:5], refs[5:]
    current_out, refs = refs[0], refs[1:]
    cos_pair, sin_pair = refs[-2:]
    width = current_ref.shape[1]
    for offset, chunk in zip(layout.offsets(), chunks_in):
        here = pl.ds(pl.multiple_of(layout.chunk_of(*offset) * rows, rows), rows)
        cos_pair[here, :] = paired(chunk[:rows, :])
        sin_pair[here, :] = paired(chunk[rows:, :])
    atoms = current_ref.shape[0]
    step = min(256, atoms)
    for at in range(0, atoms, step):
        here = slice(at, at + step)
        both = matmul(atom_tables[0][here, :], cos_pair[...])
        both = both + matmul(atom_tables[2][here, :], sin_pair[...])
        messages = both[:, :width] + both[:, width:]
        messages = messages + matmul(atom_tables[1][here, :], cos_pair[:, :width])
        messages = messages + matmul(atom_tables[3][here, :], sin_pair[:, :width])
        mean = jnp.mean(messages * messages, axis=1, keepdims=True)
        normed = messages * lax.rsqrt(mean + 1e-06) * gain[block : block + 1, :]
        hidden = product(normed, w_hidden[block]) + b_hidden[block : block + 1, :]
        hidden = hidden / (1.0 + jnp.exp(-hidden))
        current_out[here, :] = current_ref[here, :] + product(hidden, w_output[block])
    if not last:
        pair = paired(product(current_out[...], w_value[block + 1]))
        project(layout, tables, pair, refs[: layout.chunks], rows)


def vmem(count):
    return [pl.BlockSpec(memory_space=pltpu.VMEM)] * count


def call(kernel, name, outputs, scratch, limit, flops, *inputs):
    return pl.pallas_call(
        kernel,
        name=name,
        in_specs=vmem(len(inputs)),
        out_specs=vmem(len(outputs)),
        out_shape=outputs,
        scratch_shapes=scratch,
        compiler_params=pltpu.CompilerParams(vmem_limit_bytes=limit),
        cost_estimate=pl.CostEstimate(flops=flops, bytes_accessed=flops // 200, transcendentals=0),
    )(*inputs)


def local(
    layout, features, positions, wavevectors, w_value, freq_filter, norm_gain, w_hidden, b_hidden, w_output
):
    waves, channels = wavevectors.shape[1], features.shape[1]
    atoms, blocks = features.shape[0], w_value.shape[0]
    rows = waves // layout.chunks
    shape = jax.ShapeDtypeStruct
    chunk_shapes = [shape((2 * rows, channels), f32)] * layout.chunks
    index_scratch = [pltpu.VMEM((16, waves), f32), pltpu.VMEM((16, atoms), f32)]
    flops = 12 * waves * atoms * channels
    outs = call(
        lambda *refs: first_kernel(layout, rows, *refs),
        "first",
        [shape((waves, atoms), bf16)] * 4 + chunk_shapes,
        index_scratch + [pltpu.VMEM((waves, atoms), f32)],
        24 * 2**20,
        flops,
        wavevectors,
        positions,
        features,
        w_value,
    )
    tables, chunks = outs[:4], outs[4:]
    atom_tables = call(
        atom_table_kernel,
        "atom_tables",
        [shape((atoms, waves), bf16)] * 4,
        index_scratch + [pltpu.VMEM((atoms, waves), f32)],
        16 * 2**20,
        flops,
        wavevectors,
        positions,
    )
    current = features
    own_rows = layout.chunk_of(0, 0, 0) * rows
    offsets = layout.offsets()
    for block in range(blocks):
        last = block == blocks - 1
        own_filter = lax.dynamic_slice_in_dim(freq_filter[block], own_rows, rows, 0)
        scale = jnp.concatenate([own_filter, own_filter], axis=0)
        gathered = total(layout, dict(zip(offsets, chunks)), scale)
        inputs = [gathered[o] for o in offsets] + list(atom_tables)
        inputs += [current, norm_gain, w_hidden, b_hidden, w_output]
        if not last:
            inputs += [w_value] + list(tables)
        outs = call(
            lambda *refs, block=block, last=last: block_kernel(layout, rows, block, last, *refs),
            f"block_{block}",
            [shape((atoms, channels), f32)] + ([] if last else chunk_shapes),
            [pltpu.VMEM((waves, 2 * channels), bf16)] * 2,
            24 * 2**20,
            flops,
            *inputs,
        )
        current, chunks = outs[0], outs[1:]
    return current


def solution(mesh):
    placed = (
        P(("outer", "atoms"), None),
        P(None, ("outer", "atoms")),
        P(),
        P(),
        P(),
        P(),
        P(),
        P(),
        P(),
    )
    layout = Layout(mesh)

    def body(*arguments):
        return local(layout, *arguments)

    return jax.shard_map(
        body, mesh=mesh, in_specs=placed, out_specs=P(("outer", "atoms"), None), check_vma=False
    )
```

```python
import jax
import jax.numpy as jnp
from jax import lax
from jax.experimental import pallas as pl
from jax.experimental.pallas import tpu as pltpu
from jax.sharding import PartitionSpec as P

axes = ("outer", "atoms")
first_limit, table_limit, block_limit = 10 * 2**20, 8 * 2**20, 10 * 2**20
turn_bits = 18
half_sin = (0.10982699, -0.84611289, 3.60635441, -7.3082457, 4.44288292)
half_cos = (0.31069819, -1.88356299, 5.73946117, -6.97885099, 1.4142135)
to_integer = 1.5 * 2.0**23
f32, bf16 = jnp.float32, jnp.bfloat16


class Layout:
    def __init__(self, mesh):
        self.outer, self.atoms = mesh.shape["outer"], mesh.shape["atoms"]
        self.pair = 2 if self.outer % 2 == 0 else 1
        self.high = self.outer // self.pair
        self.low = 2 if self.atoms % 2 == 0 else 1
        self.line = self.atoms // self.low
        self.square = self.high * self.low
        self.chunks = self.pair * self.square

    def split(self, index):
        outer, atoms = index // self.atoms, index % self.atoms
        return outer // self.pair, outer % self.pair, atoms // self.low, atoms % self.low

    def join(self, high, pair, line, low):
        return (high * self.pair + pair) * self.atoms + line * self.low + low

    def moved(self, index, d_high, d_pair, d_line, d_low):
        high, pair, line, low = self.split(index)
        return self.join(
            (high + d_high) % self.high,
            (pair + d_pair) % self.pair,
            (line + d_line) % self.line,
            (low + d_low) % self.low,
        )

    def send(self, value, **steps):
        d = dict(d_high=0, d_pair=0, d_line=0, d_low=0) | steps
        count = self.outer * self.atoms
        return lax.ppermute(value, axes, [(i, self.moved(i, **d)) for i in range(count)])

    def exchange(self, value, bits):
        count = self.outer * self.atoms
        pairs = []
        for i in range(count):
            high, pair, line, low = self.split(i)
            pairs.append((i, self.join(high, pair, line ^ bits, low)))
        return lax.ppermute(value, axes, pairs)

    def owned(self):
        outer, atoms = lax.axis_index("outer"), lax.axis_index("atoms")
        return outer % self.pair, outer // self.pair, atoms % self.low

    def chunk_of(self, d_pair, d_high, d_low):
        pair, high, low = self.owned()
        pair = (pair + d_pair) % self.pair
        high = (high + d_high) % self.high
        low = (low + d_low) % self.low
        return (pair * self.high + high) * self.low + low

    def offsets(self):
        return [(p, h, w) for p in range(self.pair) for h in range(self.high) for w in range(self.low)]


def total(layout, parts, scale):
    squares = [(h, w) for h in range(layout.high) for w in range(layout.low)]
    held = {}
    for h, w in squares[1:] + squares[:1]:
        value = parts[0, h, w]
        for p in range(1, layout.pair):
            value = value + layout.send(parts[p, h, w], d_pair=p)
        held[h, w] = value
    own = held[0, 0]
    for h, w in squares[1:]:
        own = own + layout.send(held[h, w], d_high=h, d_low=w)
    summed = own
    if layout.line <= 4 and layout.line & (layout.line - 1) == 0:
        for d in range(layout.line - 1, 0, -1):
            summed = summed + layout.exchange(own, d)
    elif layout.line & (layout.line - 1) == 0:
        span = 1
        while span < layout.line:
            summed = summed + layout.exchange(summed, span)
            span *= 2
    else:
        for d in range(1, layout.line):
            summed = summed + layout.send(own, d_line=d)
    own = summed * scale
    out = {}
    for h, w in squares:
        value = own
        if (h, w) != (0, 0):
            value = layout.send(own, d_high=-h, d_low=-w)
        out[0, h, w] = value
        for p in range(1, layout.pair):
            out[p, h, w] = layout.send(value, d_pair=-p)
    return out


def halves(value):
    high = value.astype(bf16)
    return high, (value - high.astype(f32)).astype(bf16)


def matmul(left, right):
    return jnp.dot(left, right, preferred_element_type=f32)


def paired(value):
    high, low = halves(value)
    return jnp.concatenate([high, low], axis=1)


def product(left, right):
    width = right.shape[1]
    left_high, left_low = halves(left)
    pair = paired(right)
    both = matmul(left_high, pair)
    return both[:, :width] + both[:, width:] + matmul(left_low, pair[:, :width])


def digits(position):
    return (
        (position >> 12).astype(f32) * 2.0**-6,
        ((position >> 6) & 63).astype(f32) * 2.0**-12,
        (position & 63).astype(f32) * 2.0**-turn_bits,
    )


def operands(waves_ref, positions_ref, wave_rows, digit_rows):
    wave_rows[...] = jnp.zeros_like(wave_rows)
    digit_rows[...] = jnp.zeros_like(digit_rows)
    waves = waves_ref[...].astype(f32)
    for n, digit in enumerate(digits(positions_ref[...])):
        wave_rows[3 * n : 3 * n + 3, :] = waves
        digit_rows[3 * n : 3 * n + 3, :] = digit


def contract_rows(left, right):
    return lax.dot_general(
        left.astype(bf16), right.astype(bf16), (((0,), (0,)), ((), ())), preferred_element_type=f32
    )


def horner(coefficients, u):
    value = coefficients[0] * u + coefficients[1]
    for c in coefficients[2:]:
        value = value * u + c
    return value


def fill_tables(turns_ref, cos_high, cos_low, sin_high, sin_low):
    rows, columns = turns_ref.shape
    step, width = 32, 256

    def body(n, carry):
        here = pl.ds(pl.multiple_of(n * step, step), step)
        for at in range(0, columns, width):
            lanes = slice(at, at + width)
            turns = turns_ref[here, lanes]
            t = turns - ((turns + to_integer) - to_integer)
            u = t * t
            s = horner(half_sin, u) * t
            c = horner(half_cos, u)
            cos_high[here, lanes], cos_low[here, lanes] = halves(1.0 - s * s)
            sin_high[here, lanes], sin_low[here, lanes] = halves(s * c)
        return carry

    lax.fori_loop(0, rows // step, body, 0)


def project(layout, tables, pair, chunk_refs, rows):
    width = pair.shape[1] // 2
    for offset, chunk_ref in zip(layout.offsets(), chunk_refs):
        here = pl.ds(pl.multiple_of(layout.chunk_of(*offset) * rows, rows), rows)
        for n in range(2):
            both = matmul(tables[2 * n][here, :], pair)
            rest = matmul(tables[2 * n + 1][here, :], pair[:, :width])
            chunk_ref[n * rows : (n + 1) * rows, :] = both[:, :width] + both[:, width:] + rest


def first_kernel(layout, rows, *refs):
    sources, refs = refs[:4], refs[4:]
    tables, chunks = refs[:4], refs[4 : 4 + layout.chunks]
    wave_rows, digit_rows, turns, waves, positions, features, w_value, arrived = refs[4 + layout.chunks :]
    copies = [
        pltpu.make_async_copy(source, target, arrived.at[n])
        for n, (source, target) in enumerate(zip(sources, (waves, positions, features, w_value)))
    ]
    for copy in copies:
        copy.start()
    copies[0].wait()
    copies[1].wait()
    operands(waves, positions, wave_rows, digit_rows)
    turns[...] = contract_rows(wave_rows[...], digit_rows[...])
    fill_tables(turns, *tables)
    copies[2].wait()
    copies[3].wait()
    pair = paired(product(features[...], w_value[0]))
    project(layout, tables, pair, chunks, rows)


def atom_table_kernel(layout, rows, waves, positions, freq_filter, *refs):
    tables, scales = refs[:4], refs[4:-3]
    wave_rows, digit_rows, turns = refs[-3:]
    here = pl.ds(pl.multiple_of(layout.chunk_of(0, 0, 0) * rows, rows), rows)
    for block, scale in enumerate(scales):
        scale[:rows, :] = freq_filter[block, here, :]
        scale[rows:, :] = freq_filter[block, here, :]
    operands(waves, positions, wave_rows, digit_rows)
    turns[...] = contract_rows(digit_rows[...], wave_rows[...])
    fill_tables(turns, *tables)


def block_kernel(layout, rows, block, last, *refs):
    chunks_in, refs = refs[: layout.chunks], refs[layout.chunks :]
    atom_tables, refs = refs[:4], refs[4:]
    current_ref, gain, w_hidden, b_hidden, w_output = refs[:5]
    refs = refs[5:]
    if not last:
        w_value, tables, refs = refs[0], refs[1:5], refs[5:]
    current_out, refs = refs[0], refs[1:]
    cos_pair, sin_pair = refs[-2:]
    width = current_ref.shape[1]
    for offset, chunk in zip(layout.offsets(), chunks_in):
        here = pl.ds(pl.multiple_of(layout.chunk_of(*offset) * rows, rows), rows)
        cos_pair[here, :] = paired(chunk[:rows, :])
        sin_pair[here, :] = paired(chunk[rows:, :])
    atoms = current_ref.shape[0]
    step = min(256, atoms)
    for at in range(0, atoms, step):
        here = slice(at, at + step)
        both = matmul(atom_tables[0][here, :], cos_pair[...])
        both = both + matmul(atom_tables[2][here, :], sin_pair[...])
        messages = both[:, :width] + both[:, width:]
        messages = messages + matmul(atom_tables[1][here, :], cos_pair[:, :width])
        messages = messages + matmul(atom_tables[3][here, :], sin_pair[:, :width])
        mean = jnp.mean(messages * messages, axis=1, keepdims=True)
        normed = messages * lax.rsqrt(mean + 1e-06) * gain[block : block + 1, :]
        hidden = product(normed, w_hidden[block]) + b_hidden[block : block + 1, :]
        hidden = hidden / (1.0 + jnp.exp(-hidden))
        current_out[here, :] = current_ref[here, :] + product(hidden, w_output[block])
    if not last:
        pair = paired(product(current_out[...], w_value[block + 1]))
        project(layout, tables, pair, refs[: layout.chunks], rows)


def call(kernel, outputs, scratch, limit, flops, *inputs, space=pltpu.VMEM):
    return pl.pallas_call(
        kernel,
        in_specs=[pl.BlockSpec(memory_space=space)] * len(inputs),
        out_specs=[pl.BlockSpec(memory_space=pltpu.VMEM)] * len(outputs),
        out_shape=outputs,
        scratch_shapes=scratch,
        compiler_params=pltpu.CompilerParams(vmem_limit_bytes=limit),
        cost_estimate=pl.CostEstimate(flops=flops, bytes_accessed=flops // 200, transcendentals=0),
    )(*inputs)


def local(
    layout, features, positions, wavevectors, w_value, freq_filter, norm_gain, w_hidden, b_hidden, w_output
):
    waves, channels = wavevectors.shape[1], features.shape[1]
    atoms, blocks = features.shape[0], w_value.shape[0]
    rows = waves // layout.chunks
    shape = jax.ShapeDtypeStruct
    chunk = shape((2 * rows, channels), f32)
    index_scratch = [pltpu.VMEM((16, waves), f32), pltpu.VMEM((16, atoms), f32)]
    flops = 12 * waves * atoms * channels
    early = [wavevectors, positions, features, w_value]
    outs = call(
        lambda *refs: first_kernel(layout, rows, *refs),
        [shape((waves, atoms), bf16)] * 4 + [chunk] * layout.chunks,
        index_scratch
        + [pltpu.VMEM((waves, atoms), f32)]
        + [pltpu.VMEM(array.shape, array.dtype) for array in early]
        + [pltpu.SemaphoreType.DMA((len(early),))],
        first_limit,
        flops,
        *early,
        space=pltpu.HBM,
    )
    tables, chunks = outs[:4], outs[4:]
    outs = call(
        lambda *refs: atom_table_kernel(layout, rows, *refs),
        [shape((atoms, waves), bf16)] * 4 + [chunk] * blocks,
        index_scratch + [pltpu.VMEM((atoms, waves), f32)],
        table_limit,
        flops,
        wavevectors,
        positions,
        freq_filter,
    )
    atom_tables, scales = outs[:4], outs[4:]
    current = features
    offsets = layout.offsets()
    for block in range(blocks):
        last = block == blocks - 1
        gathered = total(layout, dict(zip(offsets, chunks)), scales[block])
        inputs = [gathered[o] for o in offsets] + list(atom_tables)
        inputs += [current, norm_gain, w_hidden, b_hidden, w_output]
        if not last:
            inputs += [w_value] + list(tables)
        outs = call(
            lambda *refs, block=block, last=last: block_kernel(layout, rows, block, last, *refs),
            [shape((atoms, channels), f32)] + ([] if last else [chunk] * layout.chunks),
            [pltpu.VMEM((waves, 2 * channels), bf16)] * 2,
            block_limit,
            flops,
            *inputs,
        )
        current, chunks = outs[0], outs[1:]
    return current


def solution(mesh):
    placed = (
        P(("outer", "atoms"), None),
        P(None, ("outer", "atoms")),
        P(),
        P(),
        P(),
        P(),
        P(),
        P(),
        P(),
    )
    layout = Layout(mesh)

    def body(*arguments):
        return local(layout, *arguments)

    return jax.shard_map(
        body, mesh=mesh, in_specs=placed, out_specs=P(("outer", "atoms"), None), check_vma=False
    )
```

```python
import jax
import jax.numpy as jnp
from jax import lax
from jax.experimental import pallas as pl
from jax.experimental.pallas import tpu as pltpu
from jax.sharding import PartitionSpec as P

axes = ("outer", "atoms")
first_limit, near_limit, table_limit, block_limit = (n * 2**20 for n in (10, 4, 8, 12))
turn_bits = 18
half_sin = (0.10982699, -0.84611289, 3.60635441, -7.3082457, 4.44288292)
half_cos = (0.31069819, -1.88356299, 5.73946117, -6.97885099, 1.4142135)
to_integer = 1.5 * 2.0**23
f32, bf16 = jnp.float32, jnp.bfloat16


class Layout:
    def __init__(self, mesh):
        self.outer, self.atoms = mesh.shape["outer"], mesh.shape["atoms"]
        self.pair = 2 if self.outer % 2 == 0 else 1
        self.high = self.outer // self.pair
        self.low = 2 if self.atoms % 2 == 0 else 1
        self.line = self.atoms // self.low
        self.square = self.high * self.low
        self.chunks = self.pair * self.square

    def split(self, index):
        outer, atoms = index // self.atoms, index % self.atoms
        return outer // self.pair, outer % self.pair, atoms // self.low, atoms % self.low

    def join(self, high, pair, line, low):
        return (high * self.pair + pair) * self.atoms + line * self.low + low

    def moved(self, index, d_high, d_pair, d_line, d_low):
        high, pair, line, low = self.split(index)
        return self.join(
            (high + d_high) % self.high,
            (pair + d_pair) % self.pair,
            (line + d_line) % self.line,
            (low + d_low) % self.low,
        )

    def send(self, value, **steps):
        d = dict(d_high=0, d_pair=0, d_line=0, d_low=0) | steps
        count = self.outer * self.atoms
        return lax.ppermute(value, axes, [(i, self.moved(i, **d)) for i in range(count)])

    def exchange(self, value, bits):
        count = self.outer * self.atoms
        pairs = []
        for i in range(count):
            high, pair, line, low = self.split(i)
            pairs.append((i, self.join(high, pair, line ^ bits, low)))
        return lax.ppermute(value, axes, pairs)

    def owned(self):
        outer, atoms = lax.axis_index("outer"), lax.axis_index("atoms")
        return outer % self.pair, outer // self.pair, atoms % self.low

    def chunk_of(self, d_pair, d_high, d_low):
        pair, high, low = self.owned()
        pair = (pair + d_pair) % self.pair
        high = (high + d_high) % self.high
        low = (low + d_low) % self.low
        return (pair * self.high + high) * self.low + low

    def offsets(self):
        return [(p, h, w) for p in range(self.pair) for h in range(self.high) for w in range(self.low)]


def total(layout, parts, scale):
    squares = [(h, w) for h in range(layout.high) for w in range(layout.low)]
    held = {}
    for h, w in squares[1:] + squares[:1]:
        value = parts[0, h, w]
        for p in range(1, layout.pair):
            value = value + layout.send(parts[p, h, w], d_pair=p)
        held[h, w] = value
    own = held[0, 0]
    for h, w in squares[1:]:
        own = own + layout.send(held[h, w], d_high=h, d_low=w)
    summed = own
    if layout.line <= 4 and layout.line & (layout.line - 1) == 0:
        for d in range(layout.line - 1, 0, -1):
            summed = summed + layout.exchange(own, d)
    elif layout.line & (layout.line - 1) == 0:
        span = 1
        while span < layout.line:
            summed = summed + layout.exchange(summed, span)
            span *= 2
    else:
        for d in range(1, layout.line):
            summed = summed + layout.send(own, d_line=d)
    own = summed * scale
    out = {}
    for h, w in squares:
        value = own
        if (h, w) != (0, 0):
            value = layout.send(own, d_high=-h, d_low=-w)
        out[0, h, w] = value
        for p in range(1, layout.pair):
            out[p, h, w] = layout.send(value, d_pair=-p)
    return out


def halves(value):
    high = value.astype(bf16)
    return high, (value - high.astype(f32)).astype(bf16)


def matmul(left, right):
    return jnp.dot(left, right, preferred_element_type=f32)


def paired(value):
    high, low = halves(value)
    return jnp.concatenate([high, low], axis=1)


def folded(value):
    width = value.shape[1] // 2
    return value[:, :width] + value[:, width:]


def stacked(weight):
    pair = paired(weight)
    width = weight.shape[1]
    again = jnp.concatenate([pair[:, :width], jnp.zeros_like(pair[:, width:])], axis=1)
    return jnp.concatenate([pair, again], axis=0)


def product(left, stack):
    return folded(matmul(paired(left), stack))


def digits(position):
    return (
        (position >> 12).astype(f32) * 2.0**-6,
        ((position >> 6) & 63).astype(f32) * 2.0**-12,
        (position & 63).astype(f32) * 2.0**-turn_bits,
    )


def operands(waves_ref, positions_ref, wave_rows, digit_rows):
    wave_rows[...] = jnp.zeros_like(wave_rows)
    digit_rows[...] = jnp.zeros_like(digit_rows)
    waves = waves_ref[...].astype(f32)
    for n, digit in enumerate(digits(positions_ref[...])):
        wave_rows[3 * n : 3 * n + 3, :] = waves
        digit_rows[3 * n : 3 * n + 3, :] = digit


def contract_rows(left, right):
    return lax.dot_general(
        left.astype(bf16), right.astype(bf16), (((0,), (0,)), ((), ())), preferred_element_type=f32
    )


def horner(coefficients, u):
    value = coefficients[0] * u + coefficients[1]
    for c in coefficients[2:]:
        value = value * u + c
    return value


def fill_tables(turns_ref, here, lanes, targets):
    turns = turns_ref[here, lanes]
    t = turns - ((turns + to_integer) - to_integer)
    u = t * t
    s = horner(half_sin, u) * t
    c = horner(half_cos, u)
    cos_high, cos_low = halves(1.0 - s * s)
    sin_high, sin_low = halves(s * c)
    for (ref, index), value in zip(targets, (cos_high, sin_high, cos_low, sin_low)):
        ref[index] = value


def fill_chunk(turns_ref, first_row, rows, table_ref, n):
    step, width = 32, 256
    for row in range(0, rows, step):
        here = pl.ds(pl.multiple_of(first_row + row, step), step)
        for at in range(0, turns_ref.shape[1], width):
            lanes = slice(at, at + width)
            targets = [
                (table_ref, (n, slice(kind * rows + row, kind * rows + row + step), lanes)) for kind in range(4)
            ]
            fill_tables(turns_ref, here, lanes, targets)


def project(table, pair, chunk_ref, rows):
    width = pair.shape[1] // 2
    both = matmul(table, pair)
    chunk_ref[...] = folded(both[: 2 * rows, :]) + both[2 * rows :, :width]


def first_kernel(layout, rows, *refs):
    sources, refs = refs[:4], refs[4:]
    far = [o for o in layout.offsets() if o[1:] != (0, 0)]
    near = [o for o in layout.offsets() if o[1:] == (0, 0)]
    table, pair_out, near_turns = refs[:3]
    chunks = refs[3 : 3 + len(far)]
    wave_rows, digit_rows, turns, waves, positions, features, w_value, arrived = refs[3 + len(far) :]
    copies = [
        pltpu.make_async_copy(source, target, arrived.at[n])
        for n, (source, target) in enumerate(zip(sources, (waves, positions, features, w_value)))
    ]
    for copy in copies:
        copy.start()
    copies[0].wait()
    copies[1].wait()
    operands(waves, positions, wave_rows, digit_rows)
    turns[...] = contract_rows(wave_rows[...], digit_rows[...])
    copies[2].wait()
    copies[3].wait()
    pair_out[...] = paired(product(features[...], stacked(w_value[0])))
    for n, offset in enumerate(near):
        here = pl.ds(pl.multiple_of(layout.chunk_of(*offset) * rows, rows), rows)
        near_turns[n * rows : (n + 1) * rows, :] = turns[here, :]
    for n, offset in enumerate(far):
        fill_chunk(turns, layout.chunk_of(*offset) * rows, rows, table, n)
        if n:
            project(table[n - 1], pair_out[...], chunks[n - 1], rows)
    project(table[len(far) - 1], pair_out[...], chunks[len(far) - 1], rows)


def near_kernel(rows, turns, pair, table, *chunks):
    for n in range(len(chunks)):
        fill_chunk(turns, n * rows, rows, table, n)
        if n:
            project(table[n - 1], pair[...], chunks[n - 1], rows)
    project(table[len(chunks) - 1], pair[...], chunks[-1], rows)


def atom_table_kernel(layout, rows, waves, positions, freq_filter, table, *refs):
    scales = refs[:-3]
    wave_rows, digit_rows, turns = refs[-3:]
    own = pl.ds(pl.multiple_of(layout.chunk_of(0, 0, 0) * rows, rows), rows)
    for block, scale in enumerate(scales):
        scale[:rows, :] = freq_filter[block, own, :]
        scale[rows:, :] = freq_filter[block, own, :]
    operands(waves, positions, wave_rows, digit_rows)
    turns[...] = contract_rows(digit_rows[...], wave_rows[...])
    atoms, count = turns.shape
    step, width = 32, 256
    half = table.shape[1] // 2
    per_group = half // step

    def body(m, carry):
        here = pl.ds(pl.multiple_of(m * step, step), step)
        group, row = m // per_group, pl.multiple_of((m % per_group) * step, step)
        for at in range(0, count, width):
            targets = [
                (table, (group, pl.ds(row + low * half, step), pl.ds(kind * count + at, width)))
                for low in range(2)
                for kind in range(2)
            ]
            fill_tables(turns, here, slice(at, at + width), targets)
        return carry

    lax.fori_loop(0, atoms // step, body, 0)


def block_kernel(layout, rows, block, last, *refs):
    chunks_in, refs = refs[: layout.chunks], refs[layout.chunks :]
    atom_table, current_ref, gain, w_hidden, b_hidden, w_output = refs[:6]
    refs = refs[6:]
    if not last:
        w_value, far_table, near_table, refs = refs[0], refs[1], refs[2], refs[3:]
    current_out, chunks_out, factor = refs[0], refs[1:-1], refs[-1]
    waves = rows * layout.chunks
    width = current_ref.shape[1]
    for offset, chunk in zip(layout.offsets(), chunks_in):
        row = pl.multiple_of(layout.chunk_of(*offset) * rows, rows)
        factor[pl.ds(row, rows), :] = paired(chunk[:rows, :])
        factor[pl.ds(waves + row, rows), :] = paired(chunk[rows:, :])
    hidden_stack, output_stack = stacked(w_hidden[block]), stacked(w_output[block])
    groups = atom_table.shape[0]
    step = atom_table.shape[1] // 2

    def back(n):
        both = matmul(atom_table[n], factor[...])
        return folded(both[:step, :]) + both[step:, :width]

    def update(n, messages):
        here = slice(n * step, (n + 1) * step)
        mean = jnp.mean(messages * messages, axis=1, keepdims=True)
        normed = messages * lax.rsqrt(mean + 1e-06) * gain[block : block + 1, :]
        hidden = product(normed, hidden_stack) + b_hidden[block : block + 1, :]
        hidden = hidden / (1.0 + jnp.exp(-hidden))
        current_out[here, :] = current_ref[here, :] + product(hidden, output_stack)

    messages = back(0)
    for n in range(groups):
        coming = back(n + 1) if n + 1 < groups else None
        update(n, messages)
        messages = coming
    if not last:
        pair = paired(product(current_out[...], stacked(w_value[block + 1])))
        far = [n for n, o in enumerate(layout.offsets()) if o[1:] != (0, 0)]
        near = [n for n, o in enumerate(layout.offsets()) if o[1:] == (0, 0)]
        for table, members in ((far_table, far), (near_table, near)):
            for at, n in enumerate(members):
                project(table[at], pair, chunks_out[n], rows)


def call(kernel, outputs, scratch, limit, flops, *inputs, space=pltpu.VMEM):
    return pl.pallas_call(
        kernel,
        in_specs=[pl.BlockSpec(memory_space=space)] * len(inputs),
        out_specs=[pl.BlockSpec(memory_space=pltpu.VMEM)] * len(outputs),
        out_shape=outputs,
        scratch_shapes=scratch,
        compiler_params=pltpu.CompilerParams(vmem_limit_bytes=limit),
        cost_estimate=pl.CostEstimate(flops=flops, bytes_accessed=flops // 200, transcendentals=0),
    )(*inputs)


def local(
    layout, features, positions, wavevectors, w_value, freq_filter, norm_gain, w_hidden, b_hidden, w_output
):
    waves, channels = wavevectors.shape[1], features.shape[1]
    atoms, blocks = features.shape[0], w_value.shape[0]
    rows = waves // layout.chunks
    shape = jax.ShapeDtypeStruct
    chunk = shape((2 * rows, channels), f32)
    index_scratch = [pltpu.VMEM((16, waves), f32), pltpu.VMEM((16, atoms), f32)]
    flops = 12 * waves * atoms * channels
    early = [wavevectors, positions, features, w_value]
    offsets = layout.offsets()
    far = [o for o in offsets if o[1:] != (0, 0)]
    near = [o for o in offsets if o[1:] == (0, 0)]
    group = min(256, atoms)
    outs = call(
        lambda *refs: first_kernel(layout, rows, *refs),
        [
            shape((len(far), 4 * rows, atoms), bf16),
            shape((atoms, 2 * channels), bf16),
            shape((len(near) * rows, atoms), f32),
        ]
        + [chunk] * len(far),
        index_scratch
        + [pltpu.VMEM((waves, atoms), f32)]
        + [pltpu.VMEM(array.shape, array.dtype) for array in early]
        + [pltpu.SemaphoreType.DMA((len(early),))],
        first_limit,
        flops,
        *[pltpu.with_memory_space_constraint(array, pltpu.HBM) for array in early],
        space=pltpu.HBM,
    )
    far_table, pair, near_turns = outs[:3]
    parts = dict(zip(far, outs[3:]))
    outs = call(
        lambda *refs: near_kernel(rows, *refs),
        [shape((len(near), 4 * rows, atoms), bf16)] + [chunk] * len(near),
        [],
        near_limit,
        flops // 4,
        near_turns,
        pair,
    )
    near_table = outs[0]
    parts |= dict(zip(near, outs[1:]))
    outs = call(
        lambda *refs: atom_table_kernel(layout, rows, *refs),
        [shape((atoms // group, 2 * group, 2 * waves), bf16)] + [chunk] * blocks,
        index_scratch + [pltpu.VMEM((atoms, waves), f32)],
        table_limit,
        flops,
        wavevectors,
        positions,
        freq_filter,
    )
    atom_table, scales = outs[0], outs[1:]
    current = features
    for block in range(blocks):
        last = block == blocks - 1
        gathered = total(layout, parts, scales[block])
        inputs = [gathered[o] for o in offsets]
        inputs += [atom_table, current, norm_gain, w_hidden, b_hidden, w_output]
        if not last:
            inputs += [w_value, far_table, near_table]
        outs = call(
            lambda *refs, block=block, last=last: block_kernel(layout, rows, block, last, *refs),
            [shape((atoms, channels), f32)] + ([] if last else [chunk] * layout.chunks),
            [pltpu.VMEM((2 * waves, 2 * channels), bf16)],
            block_limit,
            flops,
            *inputs,
        )
        current = outs[0]
        parts = dict(zip(offsets, outs[1:]))
    return current


def solution(mesh):
    placed = (
        P(("outer", "atoms"), None),
        P(None, ("outer", "atoms")),
        P(),
        P(),
        P(),
        P(),
        P(),
        P(),
        P(),
    )
    layout = Layout(mesh)

    def body(*arguments):
        return local(layout, *arguments)

    return jax.shard_map(
        body, mesh=mesh, in_specs=placed, out_specs=P(("outer", "atoms"), None), check_vma=False
    )
```

```python
import jax
import jax.numpy as jnp
from jax import lax
from jax.experimental import pallas as pl
from jax.experimental.pallas import tpu as pltpu
from jax.sharding import PartitionSpec as P

axes = ("outer", "atoms")
first_limit, near_limit, table_limit, block_limit = (n * 2**20 for n in (8, 6, 8, 12))
turn_bits = 18
half_sin = (0.10982699, -0.84611289, 3.60635441, -7.3082457, 4.44288292)
half_cos = (0.31069819, -1.88356299, 5.73946117, -6.97885099, 1.4142135)
to_integer = 1.5 * 2.0**23
f32, bf16 = jnp.float32, jnp.bfloat16


class Layout:
    def __init__(self, mesh):
        self.outer, self.atoms = mesh.shape["outer"], mesh.shape["atoms"]
        self.pair = 2 if self.outer % 2 == 0 else 1
        self.high = self.outer // self.pair
        self.low = 2 if self.atoms % 2 == 0 else 1
        self.line = self.atoms // self.low
        self.square = self.high * self.low
        self.chunks = self.pair * self.square

    def split(self, index):
        outer, atoms = index // self.atoms, index % self.atoms
        return outer // self.pair, outer % self.pair, atoms // self.low, atoms % self.low

    def join(self, high, pair, line, low):
        return (high * self.pair + pair) * self.atoms + line * self.low + low

    def moved(self, index, d_high, d_pair, d_line, d_low):
        high, pair, line, low = self.split(index)
        return self.join(
            (high + d_high) % self.high,
            (pair + d_pair) % self.pair,
            (line + d_line) % self.line,
            (low + d_low) % self.low,
        )

    def send(self, value, **steps):
        d = dict(d_high=0, d_pair=0, d_line=0, d_low=0) | steps
        count = self.outer * self.atoms
        return lax.ppermute(value, axes, [(i, self.moved(i, **d)) for i in range(count)])

    def exchange(self, value, bits):
        count = self.outer * self.atoms
        pairs = []
        for i in range(count):
            high, pair, line, low = self.split(i)
            pairs.append((i, self.join(high, pair, line ^ bits, low)))
        return lax.ppermute(value, axes, pairs)

    def owned(self):
        outer, atoms = lax.axis_index("outer"), lax.axis_index("atoms")
        return outer % self.pair, outer // self.pair, atoms % self.low

    def chunk_of(self, d_pair, d_high, d_low):
        pair, high, low = self.owned()
        pair = (pair + d_pair) % self.pair
        high = (high + d_high) % self.high
        low = (low + d_low) % self.low
        return (pair * self.high + high) * self.low + low

    def offsets(self):
        return [(p, h, w) for p in range(self.pair) for h in range(self.high) for w in range(self.low)]


def total(layout, parts, scale):
    squares = [(h, w) for h in range(layout.high) for w in range(layout.low)]
    held = {}
    for h, w in squares[1:] + squares[:1]:
        value = parts[0, h, w]
        for p in range(1, layout.pair):
            value = value + layout.send(parts[p, h, w], d_pair=p)
        held[h, w] = value
    own = held[0, 0]
    for h, w in squares[1:]:
        own = own + layout.send(held[h, w], d_high=h, d_low=w)
    summed = own
    if layout.line <= 4 and layout.line & (layout.line - 1) == 0:
        for d in range(layout.line - 1, 0, -1):
            summed = summed + layout.exchange(own, d)
    elif layout.line & (layout.line - 1) == 0:
        span = 1
        while span < layout.line:
            summed = summed + layout.exchange(summed, span)
            span *= 2
    else:
        for d in range(1, layout.line):
            summed = summed + layout.send(own, d_line=d)
    own = summed * scale
    out = {}
    for h, w in squares:
        value = own
        if (h, w) != (0, 0):
            value = layout.send(own, d_high=-h, d_low=-w)
        out[0, h, w] = value
        for p in range(1, layout.pair):
            out[p, h, w] = layout.send(value, d_pair=-p)
    return out


def halves(value):
    high = value.astype(bf16)
    return high, (value - high.astype(f32)).astype(bf16)


def matmul(left, right):
    return jnp.dot(left, right, preferred_element_type=f32)


def paired(value):
    high, low = halves(value)
    return jnp.concatenate([high, low], axis=1)


def folded(value):
    width = value.shape[1] // 2
    return value[:, :width] + value[:, width:]


def stacked(weight):
    pair = paired(weight)
    width = weight.shape[1]
    again = jnp.concatenate([pair[:, :width], jnp.zeros_like(pair[:, width:])], axis=1)
    return jnp.concatenate([pair, again], axis=0)


def product(left, stack):
    return folded(matmul(paired(left), stack))


def digits(position):
    return (
        (position >> 12).astype(f32) * 2.0**-6,
        ((position >> 6) & 63).astype(f32) * 2.0**-12,
        (position & 63).astype(f32) * 2.0**-turn_bits,
    )


def operands(waves_ref, positions_ref, wave_rows, digit_rows):
    wave_rows[...] = jnp.zeros_like(wave_rows)
    digit_rows[...] = jnp.zeros_like(digit_rows)
    waves = waves_ref[...].astype(f32)
    for n, digit in enumerate(digits(positions_ref[...])):
        wave_rows[3 * n : 3 * n + 3, :] = waves
        digit_rows[3 * n : 3 * n + 3, :] = digit


def contract_rows(left, right):
    return lax.dot_general(
        left.astype(bf16), right.astype(bf16), (((0,), (0,)), ((), ())), preferred_element_type=f32
    )


def horner(coefficients, u):
    value = coefficients[0] * u + coefficients[1]
    for c in coefficients[2:]:
        value = value * u + c
    return value


def fill_tables(turns_ref, index, targets):
    turns = turns_ref[index]
    t = turns - ((turns + to_integer) - to_integer)
    u = t * t
    s = horner(half_sin, u) * t
    c = horner(half_cos, u)
    cos_high, cos_low = halves(1.0 - s * s)
    sin_high, sin_low = halves(s * c)
    for (ref, index), value in zip(targets, (cos_high, sin_high, cos_low, sin_low)):
        ref[index] = value


def fill_chunk(wave_columns, digit_rows, turns_ref, first_row, rows, table_ref, n):
    chunk = wave_columns[pl.ds(pl.multiple_of(first_row, rows), rows), :]
    turns_ref[n] = matmul(chunk, digit_rows[...])
    step, width = 32, 256
    for row in range(0, rows, step):
        for at in range(0, digit_rows.shape[1], width):
            lanes = slice(at, at + width)
            targets = [
                (table_ref, (n, slice(kind * rows + row, kind * rows + row + step), lanes)) for kind in range(4)
            ]
            fill_tables(turns_ref, (n, slice(row, row + step), lanes), targets)


def project(table, pair, chunk_ref, rows):
    width = pair.shape[1] // 2
    both = matmul(table, pair)
    chunk_ref[...] = folded(both[: 2 * rows, :]) + both[2 * rows :, :width]


def fill_group(layout, rows, group, wave_columns, digit_rows, pair, table, chunks, turns):
    for n, offset in enumerate(group):
        row = layout.chunk_of(*offset) * rows
        fill_chunk(wave_columns, digit_rows, turns, row, rows, table, n)
        if n:
            project(table[n - 1], pair[...], chunks[n - 1], rows)
    project(table[len(group) - 1], pair[...], chunks[-1], rows)


def first_kernel(layout, rows, group, *refs):
    sources, refs = refs[:4], refs[4:]
    wave_columns, digits_out, pair, table = refs[:4]
    chunks = refs[4 : 4 + len(group)]
    wave_rows, digit_rows, turns, waves, positions, features, w_value, arrived = refs[4 + len(group) :]
    copies = [
        pltpu.make_async_copy(source, target, arrived.at[n])
        for n, (source, target) in enumerate(zip(sources, (waves, positions, features, w_value)))
    ]
    for copy in copies:
        copy.start()
    copies[0].wait()
    copies[1].wait()
    operands(waves, positions, wave_rows, digit_rows)
    count = wave_rows.shape[0]
    row, column = (lax.broadcasted_iota(jnp.int32, (count, count), axis) for axis in range(2))
    unit = (row == column).astype(f32)
    wave_columns[...] = contract_rows(wave_rows[...], unit).astype(bf16)
    digits_out[...] = digit_rows[...].astype(bf16)
    copies[2].wait()
    copies[3].wait()
    pair[...] = paired(product(features[...], stacked(w_value[0])))
    fill_group(layout, rows, group, wave_columns, digits_out, pair, table, chunks, turns)


def fill_kernel(layout, rows, group, wave_columns, digit_rows, pair, table, *refs):
    fill_group(layout, rows, group, wave_columns, digit_rows, pair, table, refs[:-1], refs[-1])


def project_kernel(rows, table, pair, *chunks):
    for n, chunk in enumerate(chunks):
        project(table[n], pair[...], chunk, rows)


def atom_table_kernel(layout, rows, waves, positions, freq_filter, table, *refs):
    scales = refs[:-3]
    wave_rows, digit_rows, turns = refs[-3:]
    own = pl.ds(pl.multiple_of(layout.chunk_of(0, 0, 0) * rows, rows), rows)
    for block, scale in enumerate(scales):
        scale[:rows, :] = freq_filter[block, own, :]
        scale[rows:, :] = freq_filter[block, own, :]
    operands(waves, positions, wave_rows, digit_rows)
    turns[...] = contract_rows(digit_rows[...], wave_rows[...])
    atoms, count = turns.shape
    step, width = 32, 256
    half = table.shape[1] // 2
    per_group = half // step

    def body(m, carry):
        here = pl.ds(pl.multiple_of(m * step, step), step)
        group, row = m // per_group, pl.multiple_of((m % per_group) * step, step)
        for at in range(0, count, width):
            targets = [
                (table, (group, pl.ds(row + low * half, step), pl.ds(kind * count + at, width)))
                for low in range(2)
                for kind in range(2)
            ]
            fill_tables(turns, (here, slice(at, at + width)), targets)
        return carry

    lax.fori_loop(0, atoms // step, body, 0)


def block_kernel(layout, rows, block, last, *refs):
    chunks_in, refs = refs[: layout.chunks], refs[layout.chunks :]
    atom_table, current_ref, gain, w_hidden, b_hidden, w_output = refs[:6]
    refs = refs[6:]
    if not last:
        w_value, table, refs = refs[0], refs[1], refs[2:]
        pair_out, refs = refs[1], refs[:1] + refs[2:]
        current_out, chunks_out, factor = refs[0], refs[1:-1], refs[-1]
    else:
        result, factor, current_out, sent = refs
    waves = rows * layout.chunks
    width = current_ref.shape[1]
    for offset, chunk in zip(layout.offsets(), chunks_in):
        row = pl.multiple_of(layout.chunk_of(*offset) * rows, rows)
        factor[pl.ds(row, rows), :] = paired(chunk[:rows, :])
        factor[pl.ds(waves + row, rows), :] = paired(chunk[rows:, :])
    hidden_stack, output_stack = stacked(w_hidden[block]), stacked(w_output[block])
    groups = atom_table.shape[0]
    step = atom_table.shape[1] // 2

    def back(n):
        both = matmul(atom_table[n], factor[...])
        return folded(both[:step, :]) + both[step:, :width]

    def update(n, messages):
        here = slice(n * step, (n + 1) * step)
        mean = jnp.mean(messages * messages, axis=1, keepdims=True)
        normed = messages * lax.rsqrt(mean + 1e-06) * gain[block : block + 1, :]
        hidden = product(normed, hidden_stack) + b_hidden[block : block + 1, :]
        hidden = hidden / (1.0 + jnp.exp(-hidden))
        current_out[here, :] = current_ref[here, :] + product(hidden, output_stack)

    messages, copies = back(0), []
    for n in range(groups):
        coming = back(n + 1) if n + 1 < groups else None
        update(n, messages)
        messages = coming
        if last:
            here = pl.ds(n * step, step)
            copies.append(pltpu.make_async_copy(current_out.at[here], result.at[here], sent.at[n]))
            copies[-1].start()
    if not last:
        pair_out[...] = paired(product(current_out[...], stacked(w_value[block + 1])))
        project_kernel(rows, table, pair_out, *chunks_out)
    for copy in copies:
        copy.wait()


def call(kernel, outputs, scratch, limit, flops, *inputs, space=pltpu.VMEM, out_space=pltpu.VMEM):
    return pl.pallas_call(
        kernel,
        in_specs=[pl.BlockSpec(memory_space=space)] * len(inputs),
        out_specs=[pl.BlockSpec(memory_space=out_space)] * len(outputs),
        out_shape=outputs,
        scratch_shapes=scratch,
        compiler_params=pltpu.CompilerParams(vmem_limit_bytes=limit),
        cost_estimate=pl.CostEstimate(flops=flops, bytes_accessed=flops // 200, transcendentals=0),
    )(*inputs)


def local(
    layout, features, positions, wavevectors, w_value, freq_filter, norm_gain, w_hidden, b_hidden, w_output
):
    waves, channels = wavevectors.shape[1], features.shape[1]
    atoms, blocks = features.shape[0], w_value.shape[0]
    rows = waves // layout.chunks
    shape = jax.ShapeDtypeStruct
    chunk = shape((2 * rows, channels), f32)
    index_scratch = [pltpu.VMEM((16, waves), f32), pltpu.VMEM((16, atoms), f32)]
    flops = 12 * waves * atoms * channels
    early = [wavevectors, positions, features, w_value]
    offsets = layout.offsets()
    squares = sorted({o[1:] for o in offsets})
    members = {"far": squares[-1:], "mid": squares[1:-1], "near": squares[:1]}
    groups = {name: [o for o in offsets if o[1:] in some] for name, some in members.items()}
    table_of = lambda name: shape((len(groups[name]), 4 * rows, atoms), bf16)
    chunks_of = lambda name: [chunk] * len(groups[name])
    turns_of = lambda name: pltpu.VMEM((len(groups[name]), rows, atoms), f32)
    pair_shape = shape((atoms, 2 * channels), bf16)
    step = min(256, atoms)
    outs = call(
        lambda *refs: first_kernel(layout, rows, groups["far"], *refs),
        [shape((waves, 16), bf16), shape((16, atoms), bf16), pair_shape, table_of("far")] + chunks_of("far"),
        index_scratch
        + [turns_of("far")]
        + [pltpu.VMEM(array.shape, array.dtype) for array in early]
        + [pltpu.SemaphoreType.DMA((len(early),))],
        first_limit,
        flops,
        *[pltpu.with_memory_space_constraint(array, pltpu.HBM) for array in early],
        space=pltpu.HBM,
    )
    wave_columns, digit_rows, pair = outs[:3]
    tables = {"far": outs[3]}
    parts = dict(zip(groups["far"], outs[4:]))
    for name in ("mid", "near"):
        outs = call(
            lambda *refs, name=name: fill_kernel(layout, rows, groups[name], *refs),
            [table_of(name)] + chunks_of(name),
            [turns_of(name)],
            near_limit,
            flops // 4,
            wave_columns,
            digit_rows,
            pair,
        )
        tables[name] = outs[0]
        parts |= dict(zip(groups[name], outs[1:]))
    outs = call(
        lambda *refs: atom_table_kernel(layout, rows, *refs),
        [shape((atoms // step, 2 * step, 2 * waves), bf16)] + [chunk] * blocks,
        index_scratch + [pltpu.VMEM((atoms, waves), f32)],
        table_limit,
        flops,
        wavevectors,
        positions,
        freq_filter,
    )
    atom_table, scales = outs[0], outs[1:]
    current = features
    for block in range(blocks):
        last = block == blocks - 1
        gathered = total(layout, parts, scales[block])
        inputs = [gathered[o] for o in offsets]
        inputs += [atom_table, current, norm_gain, w_hidden, b_hidden, w_output]
        outputs = [shape((atoms, channels), f32)]
        scratch = [pltpu.VMEM((2 * waves, 2 * channels), bf16)]
        if last:
            scratch += [pltpu.VMEM((atoms, channels), f32), pltpu.SemaphoreType.DMA((atoms // step,))]
        else:
            inputs += [w_value, tables["far"]]
            outputs += [pair_shape] + chunks_of("far")
        outs = call(
            lambda *refs, block=block, last=last: block_kernel(layout, rows, block, last, *refs),
            outputs,
            scratch,
            block_limit,
            flops,
            *inputs,
            out_space=pltpu.HBM if last else pltpu.VMEM,
        )
        current = outs[0]
        if last:
            return current
        pair, parts = outs[1], dict(zip(groups["far"], outs[2:]))
        for name in ("mid", "near"):
            outs = call(
                lambda *refs: project_kernel(rows, *refs),
                chunks_of(name),
                [],
                near_limit,
                flops // 4,
                tables[name],
                pair,
            )
            parts |= dict(zip(groups[name], outs))


def solution(mesh):
    placed = (
        P(("outer", "atoms"), None),
        P(None, ("outer", "atoms")),
        P(),
        P(),
        P(),
        P(),
        P(),
        P(),
        P(),
    )
    layout = Layout(mesh)

    def body(*arguments):
        return local(layout, *arguments)

    return jax.shard_map(body, mesh=mesh, in_specs=placed, out_specs=P(("outer", "atoms"), None), check_vma=False)
```

```python
import jax
import jax.numpy as jnp
from jax import lax
from jax.experimental import pallas as pl
from jax.experimental.pallas import tpu as pltpu
from jax.sharding import PartitionSpec as P

axes = ("outer", "atoms")
first_limit, near_limit, table_limit, block_limit = (n * 2**20 for n in (10, 4, 8, 12))
turn_bits = 18
half_sin = (0.10982699, -0.84611289, 3.60635441, -7.3082457, 4.44288292)
half_cos = (0.31069819, -1.88356299, 5.73946117, -6.97885099, 1.4142135)
to_integer = 1.5 * 2.0**23
f32, bf16 = jnp.float32, jnp.bfloat16


class Layout:
    def __init__(self, mesh):
        self.outer, self.atoms = mesh.shape["outer"], mesh.shape["atoms"]
        self.pair = 2 if self.outer % 2 == 0 else 1
        self.high = self.outer // self.pair
        self.low = 2 if self.atoms % 2 == 0 else 1
        self.line = self.atoms // self.low
        self.square = self.high * self.low
        self.chunks = self.pair * self.square

    def split(self, index):
        outer, atoms = index // self.atoms, index % self.atoms
        return outer // self.pair, outer % self.pair, atoms // self.low, atoms % self.low

    def join(self, high, pair, line, low):
        return (high * self.pair + pair) * self.atoms + line * self.low + low

    def moved(self, index, d_high, d_pair, d_line, d_low):
        high, pair, line, low = self.split(index)
        return self.join(
            (high + d_high) % self.high,
            (pair + d_pair) % self.pair,
            (line + d_line) % self.line,
            (low + d_low) % self.low,
        )

    def send(self, value, **steps):
        d = dict(d_high=0, d_pair=0, d_line=0, d_low=0) | steps
        count = self.outer * self.atoms
        return lax.ppermute(value, axes, [(i, self.moved(i, **d)) for i in range(count)])

    def exchange(self, value, bits):
        count = self.outer * self.atoms
        pairs = []
        for i in range(count):
            high, pair, line, low = self.split(i)
            pairs.append((i, self.join(high, pair, line ^ bits, low)))
        return lax.ppermute(value, axes, pairs)

    def owned(self):
        outer, atoms = lax.axis_index("outer"), lax.axis_index("atoms")
        return outer % self.pair, outer // self.pair, atoms % self.low

    def chunk_of(self, d_pair, d_high, d_low):
        pair, high, low = self.owned()
        pair = (pair + d_pair) % self.pair
        high = (high + d_high) % self.high
        low = (low + d_low) % self.low
        return (pair * self.high + high) * self.low + low

    def offsets(self):
        return [(p, h, w) for p in range(self.pair) for h in range(self.high) for w in range(self.low)]


def total(layout, parts, scale):
    squares = [(h, w) for h in range(layout.high) for w in range(layout.low)]
    held = {}
    for h, w in squares[1:] + squares[:1]:
        value = parts[0, h, w]
        for p in range(1, layout.pair):
            value = value + layout.send(parts[p, h, w], d_pair=p)
        held[h, w] = value
    own = held[0, 0]
    for h, w in squares[1:]:
        own = own + layout.send(held[h, w], d_high=h, d_low=w)
    summed = own
    if layout.line <= 4 and layout.line & (layout.line - 1) == 0:
        for d in range(layout.line - 1, 0, -1):
            summed = summed + layout.exchange(own, d)
    elif layout.line & (layout.line - 1) == 0:
        span = 1
        while span < layout.line:
            summed = summed + layout.exchange(summed, span)
            span *= 2
    else:
        for d in range(1, layout.line):
            summed = summed + layout.send(own, d_line=d)
    own = summed * scale
    out = {}
    for h, w in squares:
        value = own
        if (h, w) != (0, 0):
            value = layout.send(own, d_high=-h, d_low=-w)
        out[0, h, w] = value
        for p in range(1, layout.pair):
            out[p, h, w] = layout.send(value, d_pair=-p)
    return out


def halves(value):
    high = value.astype(bf16)
    return high, (value - high.astype(f32)).astype(bf16)


def matmul(left, right):
    return jnp.dot(left, right, preferred_element_type=f32)


def paired(value):
    high, low = halves(value)
    return jnp.concatenate([high, low], axis=1)


def folded(value):
    width = value.shape[1] // 2
    return value[:, :width] + value[:, width:]


def stacked(weight):
    pair = paired(weight)
    width = weight.shape[1]
    again = jnp.concatenate([pair[:, :width], jnp.zeros_like(pair[:, width:])], axis=1)
    return jnp.concatenate([pair, again], axis=0)


def product(left, stack):
    return folded(matmul(paired(left), stack))


def digits(position):
    return (
        (position >> 12).astype(f32) * 2.0**-6,
        ((position >> 6) & 63).astype(f32) * 2.0**-12,
        (position & 63).astype(f32) * 2.0**-turn_bits,
    )


def operands(waves_ref, positions_ref, wave_rows, digit_rows):
    wave_rows[...] = jnp.zeros_like(wave_rows)
    digit_rows[...] = jnp.zeros_like(digit_rows)
    waves = waves_ref[...].astype(f32)
    for n, digit in enumerate(digits(positions_ref[...])):
        wave_rows[3 * n : 3 * n + 3, :] = waves
        digit_rows[3 * n : 3 * n + 3, :] = digit


def contract_rows(left, right):
    return lax.dot_general(
        left.astype(bf16), right.astype(bf16), (((0,), (0,)), ((), ())), preferred_element_type=f32
    )


def horner(coefficients, u):
    value = coefficients[0] * u + coefficients[1]
    for c in coefficients[2:]:
        value = value * u + c
    return value


def fill_tables(turns_ref, here, lanes, targets):
    turns = turns_ref[here, lanes]
    t = turns - ((turns + to_integer) - to_integer)
    u = t * t
    s = horner(half_sin, u) * t
    c = horner(half_cos, u)
    cos_high, cos_low = halves(1.0 - s * s)
    sin_high, sin_low = halves(s * c)
    for (ref, index), value in zip(targets, (cos_high, sin_high, cos_low, sin_low)):
        ref[index] = value


def fill_chunk(turns_ref, first_row, rows, table_ref, n):
    step, width = 32, 256
    for row in range(0, rows, step):
        here = pl.ds(pl.multiple_of(first_row + row, step), step)
        for at in range(0, turns_ref.shape[1], width):
            lanes = slice(at, at + width)
            targets = [
                (table_ref, (n, slice(kind * rows + row, kind * rows + row + step), lanes)) for kind in range(4)
            ]
            fill_tables(turns_ref, here, lanes, targets)


def project(table, pair, chunk_ref, rows):
    width = pair.shape[1] // 2
    both = matmul(table, pair)
    chunk_ref[...] = folded(both[: 2 * rows, :]) + both[2 * rows :, :width]


def first_kernel(layout, rows, *refs):
    sources, refs = refs[:4], refs[4:]
    far = [o for o in layout.offsets() if o[1:] != (0, 0)]
    near = [o for o in layout.offsets() if o[1:] == (0, 0)]
    table, pair_out, near_turns = refs[:3]
    chunks = refs[3 : 3 + len(far)]
    wave_rows, digit_rows, turns, waves, positions, features, w_value, arrived = refs[3 + len(far) :]
    copies = [
        pltpu.make_async_copy(source, target, arrived.at[n])
        for n, (source, target) in enumerate(zip(sources, (waves, positions, features, w_value)))
    ]
    for copy in copies:
        copy.start()
    copies[0].wait()
    copies[1].wait()
    operands(waves, positions, wave_rows, digit_rows)
    turns[...] = contract_rows(wave_rows[...], digit_rows[...])
    copies[2].wait()
    copies[3].wait()
    pair_out[...] = paired(product(features[...], stacked(w_value[0])))
    for n, offset in enumerate(near):
        here = pl.ds(pl.multiple_of(layout.chunk_of(*offset) * rows, rows), rows)
        near_turns[n * rows : (n + 1) * rows, :] = turns[here, :]
    for n, offset in enumerate(far):
        fill_chunk(turns, layout.chunk_of(*offset) * rows, rows, table, n)
        if n:
            project(table[n - 1], pair_out[...], chunks[n - 1], rows)
    project(table[len(far) - 1], pair_out[...], chunks[len(far) - 1], rows)


def near_kernel(rows, turns, pair, table, *chunks):
    for n in range(len(chunks)):
        fill_chunk(turns, n * rows, rows, table, n)
        if n:
            project(table[n - 1], pair[...], chunks[n - 1], rows)
    project(table[len(chunks) - 1], pair[...], chunks[-1], rows)


def project_kernel(rows, table, pair, *chunks):
    for n, chunk in enumerate(chunks):
        project(table[n], pair[...], chunk, rows)


def atom_table_kernel(layout, rows, order, waves, positions, freq_filter, early, late, *refs):
    scales = refs[:-5]
    wave_rows, digit_rows, columns, ordered, turns = refs[-5:]
    own = pl.ds(pl.multiple_of(layout.chunk_of(0, 0, 0) * rows, rows), rows)
    for block, scale in enumerate(scales):
        scale[:rows, :] = freq_filter[block, own, :]
        scale[rows:, :] = freq_filter[block, own, :]
    operands(waves, positions, wave_rows, digit_rows)
    count = wave_rows.shape[0]
    row, column = (lax.broadcasted_iota(jnp.int32, (count, count), axis) for axis in range(2))
    columns[...] = contract_rows(wave_rows[...], (row == column).astype(f32))
    for n, offset in enumerate(order):
        first = pl.multiple_of(layout.chunk_of(*offset) * rows, rows)
        ordered[n * rows : (n + 1) * rows, :] = columns[pl.ds(first, rows), :]
    swapped = lax.dot_general(
        (row == column).astype(bf16), ordered[...].astype(bf16), (((1,), (1,)), ((), ())), preferred_element_type=f32
    )
    turns[...] = contract_rows(digit_rows[...], swapped)
    atoms, span = turns.shape[0], early.shape[2] // 2
    step = 16
    half = early.shape[1] // 2
    per_group = half // step

    def body(m, carry):
        here = pl.ds(pl.multiple_of(m * step, step), step)
        group, row = m // per_group, pl.multiple_of((m % per_group) * step, step)
        for n, table in enumerate((early, late)):
            targets = [
                (table, (group, pl.ds(row + low * half, step), slice(kind * span, (kind + 1) * span)))
                for low in range(2)
                for kind in range(2)
            ]
            fill_tables(turns, here, slice(n * span, (n + 1) * span), targets)
        return carry

    lax.fori_loop(0, atoms // step, body, 0)


def gather_factor(rows, chunks, factor):
    count = len(chunks)
    for n, chunk in enumerate(chunks):
        factor[n * rows : (n + 1) * rows, :] = paired(chunk[:rows, :])
        factor[(count + n) * rows : (count + n + 1) * rows, :] = paired(chunk[rows:, :])


def back_product(table, factor):
    both = matmul(table, factor[...])
    step, width = table.shape[0] // 2, both.shape[1] // 2
    return folded(both[:step, :]) + both[step:, :width]


def early_kernel(rows, *refs):
    chunks, (table, part, factor) = refs[:-3], refs[-3:]
    gather_factor(rows, chunks, factor)
    step = table.shape[1] // 2
    for n in range(table.shape[0]):
        part[n * step : (n + 1) * step, :] = back_product(table[n], factor)


def block_kernel(rows, count, block, last, *refs):
    chunks_in, refs = refs[:count], refs[count:]
    atom_table, part, current_ref, gain, w_hidden, b_hidden, w_output = refs[:7]
    refs = refs[7:]
    if not last:
        w_value, table, current_out, pair_out = refs[:4]
        chunks_out, factor = refs[4:-1], refs[-1]
    else:
        result, factor, current_out, sent = refs
    gather_factor(rows, chunks_in, factor)
    hidden_stack, output_stack = stacked(w_hidden[block]), stacked(w_output[block])
    groups = atom_table.shape[0]
    step = atom_table.shape[1] // 2

    def back(n):
        return back_product(atom_table[n], factor) + part[n * step : (n + 1) * step, :]

    def update(n, messages):
        here = slice(n * step, (n + 1) * step)
        mean = jnp.mean(messages * messages, axis=1, keepdims=True)
        normed = messages * lax.rsqrt(mean + 1e-06) * gain[block : block + 1, :]
        hidden = product(normed, hidden_stack) + b_hidden[block : block + 1, :]
        hidden = hidden / (1.0 + jnp.exp(-hidden))
        current_out[here, :] = current_ref[here, :] + product(hidden, output_stack)

    messages, copies = back(0), []
    for n in range(groups):
        coming = back(n + 1) if n + 1 < groups else None
        update(n, messages)
        messages = coming
        if last:
            here = pl.ds(n * step, step)
            copies.append(pltpu.make_async_copy(current_out.at[here], result.at[here], sent.at[n]))
            copies[-1].start()
    if not last:
        pair_out[...] = paired(product(current_out[...], stacked(w_value[block + 1])))
        project_kernel(rows, table, pair_out, *chunks_out)
    for copy in copies:
        copy.wait()


def call(kernel, outputs, scratch, limit, flops, *inputs, space=pltpu.VMEM, out_space=pltpu.VMEM):
    return pl.pallas_call(
        kernel,
        in_specs=[pl.BlockSpec(memory_space=space)] * len(inputs),
        out_specs=[pl.BlockSpec(memory_space=out_space)] * len(outputs),
        out_shape=outputs,
        scratch_shapes=scratch,
        compiler_params=pltpu.CompilerParams(vmem_limit_bytes=limit),
        cost_estimate=pl.CostEstimate(flops=flops, bytes_accessed=flops // 200, transcendentals=0),
    )(*inputs)


def local(
    layout, features, positions, wavevectors, w_value, freq_filter, norm_gain, w_hidden, b_hidden, w_output
):
    waves, channels = wavevectors.shape[1], features.shape[1]
    atoms, blocks = features.shape[0], w_value.shape[0]
    rows = waves // layout.chunks
    shape = jax.ShapeDtypeStruct
    chunk = shape((2 * rows, channels), f32)
    index_scratch = [pltpu.VMEM((16, waves), f32), pltpu.VMEM((16, atoms), f32)]
    flops = 12 * waves * atoms * channels
    early = [wavevectors, positions, features, w_value]
    offsets = layout.offsets()
    far = [o for o in offsets if o[1:] != (0, 0)]
    near = [o for o in offsets if o[1:] == (0, 0)]
    group = min(256, atoms)
    squares = sorted({o[1:] for o in offsets})
    early_order = [o for o in offsets if o[1:] in (squares[0], squares[-1])]
    late_order = [o for o in offsets if o not in early_order]
    outs = call(
        lambda *refs: first_kernel(layout, rows, *refs),
        [
            shape((len(far), 4 * rows, atoms), bf16),
            shape((atoms, 2 * channels), bf16),
            shape((len(near) * rows, atoms), f32),
        ]
        + [chunk] * len(far),
        index_scratch
        + [pltpu.VMEM((waves, atoms), f32)]
        + [pltpu.VMEM(array.shape, array.dtype) for array in early]
        + [pltpu.SemaphoreType.DMA((len(early),))],
        first_limit,
        flops,
        *[pltpu.with_memory_space_constraint(array, pltpu.HBM) for array in early],
        space=pltpu.HBM,
    )
    far_table, pair, near_turns = outs[:3]
    parts = dict(zip(far, outs[3:]))
    outs = call(
        lambda *refs: near_kernel(rows, *refs),
        [shape((len(near), 4 * rows, atoms), bf16)] + [chunk] * len(near),
        [],
        near_limit,
        flops // 4,
        near_turns,
        pair,
    )
    near_table = outs[0]
    parts |= dict(zip(near, outs[1:]))
    outs = call(
        lambda *refs: atom_table_kernel(layout, rows, early_order + late_order, *refs),
        [shape((atoms // group, 2 * group, 2 * rows * len(part)), bf16) for part in (early_order, late_order)]
        + [chunk] * blocks,
        index_scratch + [pltpu.VMEM((waves, 16), f32)] * 2 + [pltpu.VMEM((atoms, waves), f32)],
        table_limit,
        flops,
        wavevectors,
        positions,
        freq_filter,
    )
    early_table, late_table, scales = outs[0], outs[1], outs[2:]
    current = features
    for block in range(blocks):
        last = block == blocks - 1
        gathered = total(layout, parts, scales[block])
        part = call(
            lambda *refs: early_kernel(rows, *refs),
            [shape((atoms, channels), f32)],
            [pltpu.VMEM((2 * rows * len(early_order), 2 * channels), bf16)],
            near_limit,
            flops // 2,
            *[gathered[o] for o in early_order],
            early_table,
        )
        inputs = [gathered[o] for o in late_order]
        inputs += [late_table, part[0], current, norm_gain, w_hidden, b_hidden, w_output]
        outputs = [shape((atoms, channels), f32)]
        scratch = [pltpu.VMEM((2 * rows * len(late_order), 2 * channels), bf16)]
        if last:
            scratch += [pltpu.VMEM((atoms, channels), f32), pltpu.SemaphoreType.DMA((atoms // group,))]
        else:
            inputs += [w_value, far_table]
            outputs += [shape((atoms, 2 * channels), bf16)] + [chunk] * len(far)
        outs = call(
            lambda *refs, block=block, last=last: block_kernel(rows, len(late_order), block, last, *refs),
            outputs,
            scratch,
            block_limit,
            flops,
            *inputs,
            out_space=pltpu.HBM if last else pltpu.VMEM,
        )
        current = outs[0]
        if last:
            return current
        parts = dict(zip(far, outs[2:]))
        outs = call(
            lambda *refs: project_kernel(rows, *refs),
            [chunk] * len(near),
            [],
            near_limit,
            flops // 4,
            near_table,
            outs[1],
        )
        parts |= dict(zip(near, outs))


def solution(mesh):
    placed = (
        P(("outer", "atoms"), None),
        P(None, ("outer", "atoms")),
        P(),
        P(),
        P(),
        P(),
        P(),
        P(),
        P(),
    )
    layout = Layout(mesh)

    def body(*arguments):
        return local(layout, *arguments)

    return jax.shard_map(body, mesh=mesh, in_specs=placed, out_specs=P(("outer", "atoms"), None), check_vma=False)
```
